128 devices in a mesh: users: 4 (over z_lo, core), items: 32 (over x, y, z_hi).
Axes of the slice: x: 4, y: 4, z: 4 (z_hi: 2, z_lo: 2; z = z_hi * 2 + z_lo), core: 2. Of those that a mesh axis runs over, the one named last changes fastest.
Arguments:
- user_factors: float32 [16384, 128], P(('users', 'items')), may hold values from -1.8 to 1.8
- item_factors: float32 [65536, 128], P(('items', 'users')), may hold values from -1.8 to 1.8
- block_coords: int32 [4, 32, 256, 2], P('users', 'items'), may hold values from 0 to 31, as said below
- block_counts: int32 [4, 32], P('users', 'items'), may hold values from 32 to 256, as said below
- ratings: bfloat16 [4, 32, 256, 128, 128], P('users', 'items'), may hold values from -6 to 6
- weights: bfloat16 [4, 32, 256, 128, 128], P('users', 'items'), may hold values from 0 to 2, as said below
Outputs:
- new_users: float32 [16384, 128], P(('users', 'items'))
- new_items: float32 [65536, 128], P(('items', 'users'))
The draws below stay inside these ranges and needn't reach their ends.
Inputs may be any that keep to these rules, and one draw needn't show every extreme that they name: `block_coords`: within one group and shard the 256 slots name distinct pairs of user block and item block, also the slots that are not live. `block_counts`: some group and shard has all 256 slots live in every draw. `weights`: zero marks an unobserved rating.
All inputs are finite; a program needn't handle non-finite values.
Results may differ from the reference program's by a relative error of at most 0.002.
Values may be sent and summed in bfloat16 or wider, within the bound.
A program may use at most 192 MiB of HBM per device.

```python
import jax
import jax.numpy as jnp
from jax import lax

R = 128
B = 128
UBLK = 32
IBLK = 16
NB = 256
STEPS = 2
USER_CLUSTERS = 4
SHARDS = 32
NU = 16384
NI = 65536


def draw_block_coords(key, part):
    device_keys = jax.random.split(key, USER_CLUSTERS * SHARDS)
    cells = jax.vmap(lambda one_key: jax.random.permutation(one_key, UBLK * IBLK)[:NB])(device_keys)
    cells = cells.astype(jnp.int32)
    pairs = jnp.stack([cells // IBLK, cells % IBLK], axis=-1)
    return pairs.reshape(USER_CLUSTERS, SHARDS, NB, 2).astype(jnp.int32)


def draw_block_counts(key, part):
    left_draw = jax.random.randint(jax.random.fold_in(key, 11), (USER_CLUSTERS, SHARDS), 0, NB + 1, dtype=jnp.int32)
    right_draw = jax.random.randint(jax.random.fold_in(key, 12), (USER_CLUSTERS, SHARDS), 0, NB + 1, dtype=jnp.int32)
    counts_drawn = jnp.maximum(max(1, NB // 8), left_draw * right_draw // NB)
    busiest = jax.random.randint(jax.random.fold_in(key, 13), (), 0, USER_CLUSTERS * SHARDS, dtype=jnp.int32)
    device_ids = jnp.arange(USER_CLUSTERS * SHARDS, dtype=jnp.int32).reshape(USER_CLUSTERS, SHARDS)
    return jnp.where(device_ids == busiest, NB, counts_drawn).astype(jnp.int32)


def draw_weights(key, part):
    full_shape = (USER_CLUSTERS, SHARDS, NB, B, B)
    chosen = jax.random.uniform(jax.random.fold_in(key, 21), full_shape)
    levels = jnp.exp(jax.random.uniform(jax.random.fold_in(key, 22), full_shape, minval=jnp.log(0.5), maxval=jnp.log(2.0)))
    keep_share = 0.5
    return jnp.where(chosen < keep_share, 0.0, levels).astype(jnp.float32).astype(jnp.bfloat16)


def block_levels(key, dims, shards, low, largest):
    loudness, own = 1.0, jax.random.fold_in(key, 6)
    for dim, parts in shards:
        draws = jnp.exp(jax.random.uniform(jax.random.fold_in(own, dim), (parts,), jnp.float32, low / len(shards), largest / len(shards)))
        loudness = loudness * jnp.repeat(draws, dims[dim] // parts).reshape([-1 if axis == dim else 1 for axis in range(len(dims))])
    return loudness


def scatter_about(stream_key, shape, deviation, most, cuts=(), held_as=jnp.bfloat16):
    level = block_levels(stream_key, shape, cuts, -0.22, 0.18) if cuts else 1.0
    array = jax.random.normal(stream_key, shape, jnp.float32) * deviation * level
    return jnp.minimum(jnp.maximum(array, -most), most).astype(held_as)


def setup_inputs(seed: int = 0) -> dict:
    seeds = jax.random.split(jax.random.key(seed), 7)
    user_factors = scatter_about(seeds[0], (NU, R), 0.3, 1.8, ((0, 128),), jnp.float32)
    item_factors = scatter_about(seeds[1], (NI, R), 0.3, 1.8, ((0, 128),), jnp.float32)
    block_coords = draw_block_coords(jax.random.fold_in(seeds[6], 71), 0)
    block_counts = draw_block_counts(jax.random.fold_in(seeds[6], 71), 0)
    ratings = scatter_about(seeds[4], (USER_CLUSTERS, SHARDS, NB, B, B), 1.0, 6.0, ((0, 4), (1, 32)))
    weights = draw_weights(jax.random.fold_in(seeds[6], 71), 0)
    return dict(user_factors=user_factors, item_factors=item_factors, block_coords=block_coords, block_counts=block_counts, ratings=ratings, weights=weights)


def block_terms(user_tiles, item_tiles, user_index, item_index, slot_live, ratings, weights):
    user_factor_rows = user_tiles[user_index].astype(jnp.float32)
    item_factor_rows = item_tiles[item_index].astype(jnp.float32)
    predicted_ratings = jnp.einsum("ijq,ieq->ije", user_factor_rows, item_factor_rows)
    residual_errors = weights.astype(jnp.float32) * (predicted_ratings - ratings.astype(jnp.float32))
    residual_errors = jnp.where(slot_live[:, None, None], residual_errors, jnp.float32(0.0)).astype(jnp.bfloat16)
    residual_errors = lax.optimization_barrier(residual_errors).astype(jnp.float32)
    user_gradient_terms = jnp.einsum("tcj,tjz->tcz", residual_errors, item_factor_rows)
    item_gradient_terms = jnp.einsum("lxc,lxo->lco", residual_errors, user_factor_rows)
    return user_gradient_terms, item_gradient_terms


def reference(user_factors, item_factors, block_coords, block_counts, ratings, weights):
    for position in range(STEPS):
        user_tiles = user_factors.astype(jnp.bfloat16).reshape(USER_CLUSTERS * UBLK, B, R)
        item_tiles = item_factors.astype(jnp.bfloat16).reshape(SHARDS * IBLK, B, R)

        def device_step(totals, device):
            group = device // SHARDS
            shard = device % SHARDS
            coords = block_coords[group, shard]
            user_index = (group * UBLK + coords[:, 0]).astype(jnp.int32)
            item_index = (shard * IBLK + coords[:, 1]).astype(jnp.int32)
            slot_live = jnp.arange(NB, dtype=jnp.int32) < block_counts[group, shard]
            user_gradient_terms, item_gradient_terms = block_terms(user_tiles, item_tiles, user_index, item_index, slot_live, ratings[group, shard], weights[group, shard])
            return (totals[0].at[user_index].add(user_gradient_terms), totals[1].at[item_index].add(item_gradient_terms)), None

        start_sums = (jnp.zeros((USER_CLUSTERS * UBLK, B, R), jnp.float32), jnp.zeros((SHARDS * IBLK, B, R), jnp.float32))
        totals, unused = lax.scan(device_step, start_sums, jnp.arange(USER_CLUSTERS * SHARDS, dtype=jnp.int32))
        user_grad = totals[0].reshape(NU, R)
        item_grad = totals[1].reshape(NI, R)
        user_factors, item_factors = user_factors - (20.0 / NI) * user_grad, item_factors - (20.0 / NU) * item_grad
    return user_factors, item_factors
```

```python
import functools

import jax
import jax.numpy as jnp
from jax import lax
from jax.experimental import pallas as pl
from jax.experimental.pallas import tpu as pltpu
from jax.sharding import PartitionSpec as P

BF = jnp.bfloat16
F32 = jnp.float32
MESH = pl.DeviceIdType.MESH

TILE = 128
RANK = 128
STEPS = 2
SLOTS = 256
ITEM_BLOCKS = 16
USER_RATE = 20.0 / 65536
ITEM_RATE = 20.0 / 16384


def contract(a, b, da, db):
    return lax.dot_general(a, b, (((da,), (db,)), ((), ())), preferred_element_type=F32)


def kernel(
    users_ref, items_ref, coords_ref, counts_ref, ratings_hbm, weights_hbm,
    new_users_ref, new_items_ref,
    ratings, weights, table_v, table_s,
    user_tab, item_tab, user_pair, user_master, item_master,
    grad_send, grad_own, ring_far, near_send, ring_near, pair_send, pair_recv,
    item_grad, core_send, core_recv, item_sum, zl_send, zl_recv,
    load_sem, pair_ss, pair_rs, agn_ss, agn_rs, agf_ss, agf_rs, rsf_ss, rsf_rs,
    rsn_ss, rsn_rs, core_ss, core_rs, zl_ss, zl_rs, agi_ss, agi_rs,
):
    me_u = lax.axis_index("users")
    me_i = lax.axis_index("items")
    core = me_u % 2
    zlo = me_u // 2
    x = me_i // 8
    y = (me_i // 2) % 4
    zh = me_i % 2
    near = x + core * (y - x)
    far = y + core * (x - y)
    near_stride = 8 - 6 * core
    far_stride = 2 + 6 * core

    def near_peer(r):
        return (me_u, me_i + ((near + r) % 4 - near) * near_stride)

    def far_peer(r):
        return (me_u, me_i + ((far + r) % 4 - far) * far_stride)

    pair_peer = (me_u, me_i + 1 - 2 * zh)
    core_peer = (me_u + 1 - 2 * core, me_i)
    zlo_peer = (me_u + 2 - 4 * zlo, me_i)

    def remote(src, dst, ss, rs, peer):
        return pltpu.make_async_remote_copy(
            src_ref=src, dst_ref=dst, send_sem=ss, recv_sem=rs, device_id=peer, device_id_type=MESH
        )

    loads = (
        pltpu.make_async_copy(ratings_hbm.at[0, 0], ratings.at[pl.ds(0, SLOTS)], load_sem.at[0]),
        pltpu.make_async_copy(weights_hbm.at[0, 0], weights.at[pl.ds(0, SLOTS)], load_sem.at[1]),
    )
    for copy in loads:
        copy.start()

    peers = [near_peer(r) for r in (1, 2, 3)] + [far_peer(r) for r in (1, 2, 3)]
    peers += [pair_peer, core_peer, zlo_peer]
    barrier = pltpu.get_barrier_semaphore()
    for peer in peers:
        pl.semaphore_signal(barrier, inc=1, device_id=peer, device_id_type=MESH)
    pl.semaphore_wait(barrier, len(peers))

    def pair_copy(step):
        if step == 0:
            return remote(users_ref, user_pair, pair_ss.at[0], pair_rs.at[0], pair_peer)
        if step == 1:
            return remote(pair_send.at[0], pair_recv.at[0], pair_ss.at[1], pair_rs.at[1], pair_peer)
        return remote(
            pair_send.at[1, 1 - zh], pair_recv.at[1, 1 - zh], pair_ss.at[2], pair_rs.at[2], pair_peer
        )

    def gather_near(step, r):
        piece = user_tab.at[step, far, near]
        return remote(piece, piece, agn_ss.at[step, r - 1], agn_rs.at[step, r - 1], near_peer(r))

    def gather_far(step, r, n):
        piece = user_tab.at[step, far, n]
        return remote(piece, piece, agf_ss.at[step, r - 1, n], agf_rs.at[step, r - 1, n], far_peer(r))

    def reduce_far(step, r, h):
        return remote(
            grad_send.at[step, r - 1, h], ring_far.at[step, r - 1, h],
            rsf_ss.at[step, r - 1, h], rsf_rs.at[step, r - 1, h], far_peer(r),
        )

    def reduce_near(step, r):
        return remote(
            near_send.at[step, (near + r) % 4], ring_near.at[step, r - 1],
            rsn_ss.at[step, r - 1], rsn_rs.at[step, r - 1], near_peer(r),
        )

    def reduce_core(step):
        return remote(core_send.at[step], core_recv.at[step], core_ss.at[step], core_rs.at[step], core_peer)

    def reduce_zlo(step):
        return remote(zl_send.at[step], zl_recv.at[step], zl_ss.at[step], zl_rs.at[step], zlo_peer)

    def gather_items(step, k):
        quarter = me_u if k < 2 else me_u + 2 - 4 * zlo
        piece = item_tab.at[step, quarter]
        return remote(
            piece, piece, agi_ss.at[step, k], agi_rs.at[step, k], zlo_peer if k == 0 else core_peer
        )

    def send_users(step):
        for r in (1, 3, 2):
            gather_near(step, r).start()
        for r in (1, 3, 2):
            gather_far(step, r, near).start()

    def forward_users(step, r):
        gather_near(step, r).wait_recv()
        n = (near + 4 - r) % 4
        for k in (1, 3, 2):
            gather_far(step, k, n).start()

    def send_items(step):
        gather_items(step, 0).start()
        gather_items(step, 1).start()

    pair_copy(0).start()
    item_master[...] = items_ref[...]
    item_tab[0, me_u] = items_ref[...].astype(BF)
    send_items(0)

    coords = coords_ref[0, 0]
    cell = coords[:, 0:1] * ITEM_BLOCKS + coords[:, 1:2]
    slot = lax.broadcasted_iota(jnp.int32, (SLOTS, 512), 0)
    hit = (cell == lax.broadcasted_iota(jnp.int32, (SLOTS, 512), 1)) & (slot < counts_ref[0, 0])
    table_v[...] = SLOTS + jnp.sum(jnp.where(hit, slot - SLOTS, 0), axis=0, keepdims=True)
    to_scalars = pltpu.make_async_copy(table_v, table_s, load_sem.at[2])
    to_scalars.start()
    ratings[SLOTS] = jnp.zeros((TILE, TILE), BF)
    weights[SLOTS] = jnp.zeros((TILE, TILE), BF)

    pair_copy(0).wait_recv()
    user_master[zh] = users_ref[...]
    user_master[1 - zh] = user_pair[...]
    user_tab[0, far, near] = user_master[...].astype(BF)
    send_users(0)
    to_scalars.wait()

    own_half = near // 2
    mate = 3 - 2 * (near % 2)

    for step in range(STEPS):
        gather_items(step, 0).wait_recv()
        gather_items(step, 2).start()
        gather_items(step, 1).wait_recv()
        if step == 0:
            for copy in loads:
                copy.wait()
        gather_items(step, 2).wait_recv()
        item_grad[...] = jnp.zeros_like(item_grad)

        def part(c, carry):
            rel = ((c + 1) // 2) % 4
            flip = (c + 1) % 2

            @pl.when(c == 0)
            def _():
                forward_users(step, mate)

            @pl.when(c == 1)
            def _():
                forward_users(step, 2)
                forward_users(step, 4 - mate)

            half = jnp.where(rel == 0, (own_half + 1 + flip) % 2, (own_half + flip) % 2)
            chunk = (far + rel) % 4

            @pl.when(rel > 0)
            def _():
                for k in range(2):
                    gather_far(step, 4 - rel, 2 * half + k).wait_recv()

            u = user_tab[step, chunk, pl.ds(2 * half, 2)].reshape(4 * TILE, RANK)
            v = item_tab[step].reshape(ITEM_BLOCKS * TILE, RANK)
            scores = contract(u, v, 1, 1)
            rows = []
            for a in range(4):
                block = (2 * half + a // 2) * near_stride + chunk * far_stride + a % 2
                cols = []
                for b in range(ITEM_BLOCKS):
                    k = table_s[0, block * ITEM_BLOCKS + b]
                    score = scores[a * TILE:(a + 1) * TILE, b * TILE:(b + 1) * TILE]
                    err = weights[k].astype(F32) * (score - ratings[k].astype(F32))
                    cols.append(err.astype(BF))
                rows.append(jnp.concatenate(cols, axis=1))
            errors = jnp.concatenate(rows, axis=0)
            user_part = contract(errors, v, 1, 0)
            item_part = contract(u, errors, 0, 0)
            for q in range(4):
                item_grad[q] += item_part[:, q * 512:(q + 1) * 512]

            @pl.when(rel == 0)
            def _():
                grad_own[half] = user_part

            @pl.when(rel > 0)
            def _():
                grad_send[step, rel - 1, half] = user_part.astype(BF)
                reduce_far(step, rel, half).start()

            return carry

        lax.fori_loop(0, 8, part, 0)

        for z in range(2):
            core_send[step, z] = item_grad[2 * z + 1 - core].astype(BF)
        reduce_core(step).start()

        for h in range(2):
            for r in (1, 2, 3):
                reduce_far(step, r, h).wait_recv()
            total = grad_own[h]
            for r in range(3):
                total = total + ring_far[step, r, h].astype(F32)
            grad_own[h] = total
            near_send[step, pl.ds(2 * h, 2)] = total.astype(BF).reshape(2, 2 * TILE, RANK)
        for r in (1, 3, 2):
            reduce_near(step, r).start()

        reduce_core(step).wait_recv()
        for z in range(2):
            item_sum[z] = item_grad[2 * z + core] + core_recv[step, z].astype(F32)
        zl_send[step] = item_sum[1 - zlo].astype(BF)
        reduce_zlo(step).start()

        for r in (1, 2, 3):
            reduce_near(step, r).wait_recv()
        total = grad_own[near // 2, pl.ds(pl.multiple_of((near % 2) * 256, 256), 256)]
        for r in range(3):
            total = total + ring_near[step, r].astype(F32)
        pair_send[step] = total.astype(BF).reshape(2, TILE, RANK)
        pair_copy(step + 1).start()

        reduce_zlo(step).wait_recv()
        item_total = (item_sum[zlo] + zl_recv[step].astype(F32)).T
        new_rows = item_master[...] - ITEM_RATE * item_total
        if step + 1 < STEPS:
            item_master[...] = new_rows
            item_tab[step + 1, me_u] = new_rows.astype(BF)
            send_items(step + 1)
        else:
            new_items_ref[...] = new_rows

        pair_copy(step + 1).wait_recv()
        if step + 1 < STEPS:
            both = pair_send[step].astype(F32) + pair_recv[step].astype(F32)
            user_master[...] = user_master[...] - USER_RATE * both
            user_tab[step + 1, far, near] = user_master[...].astype(BF)
            send_users(step + 1)
        else:
            grad_own[0, 0:256] = total
            mine = grad_own[0, pl.ds(pl.multiple_of(zh * TILE, TILE), TILE)]
            mine = mine + pair_recv[step, zh].astype(F32)
            new_users_ref[...] = user_master[zh] - USER_RATE * mine

    for step in range(STEPS):
        for r in (1, 2, 3):
            gather_near(step, r).wait_send()
            for n in range(4):
                gather_far(step, r, n).wait_send()
            for h in range(2):
                reduce_far(step, r, h).wait_send()
            reduce_near(step, r).wait_send()
        reduce_core(step).wait_send()
        reduce_zlo(step).wait_send()
        for k in range(3):
            gather_items(step, k).wait_send()
    for step in range(STEPS + 1):
        pair_copy(step).wait_send()


def per_device(users, items, coords, counts, ratings, weights):
    vmem = pl.BlockSpec(memory_space=pltpu.VMEM)
    hbm = pl.BlockSpec(memory_space=pl.ANY)
    dma = pltpu.SemaphoreType.DMA
    return pl.pallas_call(
        kernel,
        name="factorize",
        out_shape=(
            jax.ShapeDtypeStruct(users.shape, F32),
            jax.ShapeDtypeStruct(items.shape, F32),
        ),
        in_specs=[vmem, vmem, vmem, pl.BlockSpec(memory_space=pltpu.SMEM), hbm, hbm],
        out_specs=(vmem, vmem),
        scratch_shapes=[
            pltpu.VMEM((SLOTS + 1, TILE, TILE), BF),
            pltpu.VMEM((SLOTS + 1, TILE, TILE), BF),
            pltpu.VMEM((1, 512), jnp.int32),
            pltpu.SMEM((1, 512), jnp.int32),
            pltpu.VMEM((STEPS, 4, 4, 2, TILE, RANK), BF),
            pltpu.VMEM((STEPS, 4, 512, RANK), BF),
            pltpu.VMEM((TILE, RANK), F32),
            pltpu.VMEM((2, TILE, RANK), F32),
            pltpu.VMEM((512, RANK), F32),
            pltpu.VMEM((STEPS, 3, 2, 512, RANK), BF),
            pltpu.VMEM((2, 512, RANK), F32),
            pltpu.VMEM((STEPS, 3, 2, 512, RANK), BF),
            pltpu.VMEM((STEPS, 4, 256, RANK), BF),
            pltpu.VMEM((STEPS, 3, 256, RANK), BF),
            pltpu.VMEM((STEPS, 2, TILE, RANK), BF),
            pltpu.VMEM((STEPS, 2, TILE, RANK), BF),
            pltpu.VMEM((4, RANK, 512), F32),
            pltpu.VMEM((STEPS, 2, RANK, 512), BF),
            pltpu.VMEM((STEPS, 2, RANK, 512), BF),
            pltpu.VMEM((2, RANK, 512), F32),
            pltpu.VMEM((STEPS, RANK, 512), BF),
            pltpu.VMEM((STEPS, RANK, 512), BF),
            dma((3,)),
            dma((STEPS + 1,)), dma((STEPS + 1,)),
            dma((STEPS, 3)), dma((STEPS, 3)),
            dma((STEPS, 3, 4)), dma((STEPS, 3, 4)),
            dma((STEPS, 3, 2)), dma((STEPS, 3, 2)),
            dma((STEPS, 3)), dma((STEPS, 3)),
            dma((STEPS,)), dma((STEPS,)),
            dma((STEPS,)), dma((STEPS,)),
            dma((STEPS, 3)), dma((STEPS, 3)),
        ],
        compiler_params=pltpu.CompilerParams(
            collective_id=0, has_side_effects=True, vmem_limit_bytes=60 * 2**20
        ),
        cost_estimate=pl.CostEstimate(
            flops=STEPS * 3 * 2 * 512 * TILE**3, bytes_accessed=2 * SLOTS * TILE * TILE * 2, transcendentals=0
        ),
    )(users, items, coords, counts, ratings, weights)


def solution(mesh):
    return jax.shard_map(
        per_device,
        mesh=mesh,
        in_specs=(
            P(("users", "items"), None),
            P(("items", "users"), None),
            P("users", "items", None, None),
            P("users", "items"),
            P("users", "items", None, None, None),
            P("users", "items", None, None, None),
        ),
        out_specs=(P(("users", "items"), None), P(("items", "users"), None)),
        check_vma=False,
    )
```

```python
import functools

import jax
import jax.numpy as jnp
from jax import lax
from jax.experimental import pallas as pl
from jax.experimental.pallas import tpu as pltpu
from jax.sharding import PartitionSpec as P

BF = jnp.bfloat16
F32 = jnp.float32
MESH = pl.DeviceIdType.MESH

TILE = 128
RANK = 128
STEPS = 2
SLOTS = 256
ITEM_BLOCKS = 16
USER_RATE = 20.0 / 65536
ITEM_RATE = 20.0 / 16384
LATE = 7


def contract(a, b, da, db):
    return lax.dot_general(a, b, (((da,), (db,)), ((), ())), preferred_element_type=F32)


def kernel(
    users_hbm, items_hbm, coords_hbm, counts_ref, ratings_hbm, weights_hbm,
    new_users_hbm, new_items_hbm,
    ratings, weights, coords, table_v, table_s,
    user_tab, item_tab, user_pair, user_master, item_master,
    grad_send, grad_own, ring_far, near_send, near_own, ring_near, pair_send, pair_recv,
    item_grad, core_send, core_recv, item_sum, zl_send, zl_recv,
    load_sem, pair_ss, pair_rs, agn_ss, agn_rs, agf_ss, agf_rs, rsf_ss, rsf_rs,
    rsn_ss, rsn_rs, core_ss, core_rs, zl_ss, zl_rs, agi_ss, agi_rs,
):
    me_u = lax.axis_index("users")
    me_i = lax.axis_index("items")
    core = me_u % 2
    zlo = me_u // 2
    x = me_i // 8
    y = (me_i // 2) % 4
    zh = me_i % 2
    near = x + core * (y - x)
    far = y + core * (x - y)
    near_stride = 8 - 6 * core
    far_stride = 2 + 6 * core

    def near_peer(r):
        return (me_u, me_i + ((near + r) % 4 - near) * near_stride)

    def far_peer(r):
        return (me_u, me_i + ((far + r) % 4 - far) * far_stride)

    pair_peer = (me_u, me_i + 1 - 2 * zh)
    core_peer = (me_u + 1 - 2 * core, me_i)
    zlo_peer = (me_u + 2 - 4 * zlo, me_i)

    def remote(src, dst, ss, rs, peer):
        return pltpu.make_async_remote_copy(
            src_ref=src, dst_ref=dst, send_sem=ss, recv_sem=rs, device_id=peer, device_id_type=MESH
        )

    load_items = pltpu.make_async_copy(items_hbm, item_master, load_sem.at[0])
    load_users = pltpu.make_async_copy(users_hbm, user_master.at[zh], load_sem.at[1])
    load_coords = pltpu.make_async_copy(coords_hbm.at[0, 0], coords, load_sem.at[2])
    load_items.start()
    load_users.start()
    load_coords.start()
    loads = (
        pltpu.make_async_copy(ratings_hbm.at[0, 0], ratings.at[pl.ds(0, SLOTS)], load_sem.at[3]),
        pltpu.make_async_copy(weights_hbm.at[0, 0], weights.at[pl.ds(0, SLOTS)], load_sem.at[4]),
    )
    for copy in loads:
        copy.start()
    to_scalars = pltpu.make_async_copy(table_v, table_s, load_sem.at[5])
    store_items = pltpu.make_async_copy(item_master, new_items_hbm, load_sem.at[6])
    store_users = pltpu.make_async_copy(user_pair, new_users_hbm, load_sem.at[7])

    peers = [near_peer(r) for r in (1, 2, 3)] + [far_peer(r) for r in (1, 2, 3)]
    peers += [pair_peer, core_peer, zlo_peer]
    barrier = pltpu.get_barrier_semaphore()
    for peer in peers:
        pl.semaphore_signal(barrier, inc=1, device_id=peer, device_id_type=MESH)
    pl.semaphore_wait(barrier, len(peers))

    def pair_rows():
        return remote(users_hbm, user_pair, pair_ss.at[0, 0], pair_rs.at[0, 0], pair_peer)

    def pair_sums(z):
        return remote(
            pair_send.at[0, z], pair_recv.at[0, z], pair_ss.at[1, z], pair_rs.at[1, z], pair_peer
        )

    def pair_last():
        return remote(
            pair_send.at[1, 1 - zh], pair_recv.at[1, 1 - zh], pair_ss.at[0, 1], pair_rs.at[0, 1], pair_peer
        )

    def gather_near(step, r, z):
        piece = user_tab.at[step, far, z, near]
        return remote(
            piece, piece, agn_ss.at[step, r - 1, z], agn_rs.at[step, r - 1, z], near_peer(r)
        )

    def gather_far(step, r, z):
        piece = user_tab.at[step, far, z]
        return remote(piece, piece, agf_ss.at[step, r - 1, z], agf_rs.at[step, r - 1, z], far_peer(r))

    def reduce_far(step, r, z):
        return remote(
            grad_send.at[step, r - 1, z], ring_far.at[step, r - 1, z],
            rsf_ss.at[step, r - 1, z], rsf_rs.at[step, r - 1, z], far_peer(r),
        )

    def reduce_near(step, r, z):
        return remote(
            near_send.at[step, z, (near + r) % 4], ring_near.at[step, z, r - 1],
            rsn_ss.at[step, r - 1, z], rsn_rs.at[step, r - 1, z], near_peer(r),
        )

    def reduce_core(step):
        return remote(core_send.at[step], core_recv.at[step], core_ss.at[step], core_rs.at[step], core_peer)

    def reduce_zlo(step):
        return remote(zl_send.at[step], zl_recv.at[step], zl_ss.at[step], zl_rs.at[step], zlo_peer)

    def gather_items(step, k):
        quarter = me_u if k < 2 else me_u + 2 - 4 * zlo
        piece = item_tab.at[step, quarter]
        return remote(
            piece, piece, agi_ss.at[step, k], agi_rs.at[step, k], zlo_peer if k == 0 else core_peer
        )

    def send_users(step, z):
        user_tab[step, far, z, near] = user_master[z].astype(BF)
        for r in (2, 1, 3):
            gather_near(step, r, z).start()

    def forward_users(step, z):
        for r in (1, 3, 2):
            gather_near(step, r, z).wait_recv()
        for r in (3, 2, 1):
            gather_far(step, r, z).start()

    def send_items(step):
        item_tab[step, me_u] = item_master[...].astype(BF)
        gather_items(step, 0).start()
        gather_items(step, 1).start()

    def sum_far(step, z):
        for r in (1, 2, 3):
            reduce_far(step, r, z).wait_recv()
        total = grad_own[z]
        for r in range(3):
            total = total + ring_far[step, r, z].astype(F32)
        near_own[z] = total.reshape(4, TILE, RANK)
        near_send[step, z] = total.astype(BF).reshape(4, TILE, RANK)
        for r in (2, 1, 3):
            reduce_near(step, r, z).start()

    def sum_near(step, z):
        for r in (1, 3, 2):
            reduce_near(step, r, z).wait_recv()
        total = near_own[z, near]
        for r in range(3):
            total = total + ring_near[step, z, r].astype(F32)
        near_own[z, near] = total
        pair_send[step, z] = total.astype(BF)

    def update_users(z):
        pair_sums(z).wait_recv()
        both = pair_send[0, z].astype(F32) + pair_recv[0, z].astype(F32)
        user_master[z] = user_master[z] - USER_RATE * both

    pair_rows().start()
    load_items.wait()
    send_items(0)

    load_coords.wait()
    cell = coords[0:1] * ITEM_BLOCKS + coords[1:2]
    cell = jnp.where(lax.broadcasted_iota(jnp.int32, (1, SLOTS), 1) < counts_ref[0, 0], cell, -1)
    cell = jnp.broadcast_to(cell, (8, SLOTS)).T[:, 0:1]
    slot = lax.broadcasted_iota(jnp.int32, (SLOTS, 512), 0)
    hit = cell == lax.broadcasted_iota(jnp.int32, (SLOTS, 512), 1)
    table_v[...] = SLOTS + jnp.sum(jnp.where(hit, slot - SLOTS, 0), axis=0, keepdims=True)
    to_scalars.start()
    ratings[SLOTS] = jnp.zeros((TILE, TILE), BF)
    weights[SLOTS] = jnp.zeros((TILE, TILE), BF)

    load_users.wait()
    pair_rows().wait_recv()
    user_master[1 - zh] = user_pair[...]
    for z in range(2):
        send_users(0, z)
    gather_items(0, 0).wait_recv()
    gather_items(0, 2).start()
    for z in range(2):
        forward_users(0, z)
    to_scalars.wait()
    gather_items(0, 1).wait_recv()
    gather_items(0, 2).wait_recv()
    for copy in loads:
        copy.wait()

    for step in range(STEPS):
        last = step + 1 == STEPS
        item_grad[...] = jnp.zeros_like(item_grad)

        def part(c, carry):
            z = c // 4
            rel = (c % 4 + z) % 4
            chunk = (far + rel) % 4

            if step > 0:
                @pl.when(c == 1)
                def _():
                    forward_users(step, 1)

            @pl.when(c == LATE)
            def _():
                sum_far(step, 0)

            @pl.when(rel > 0)
            def _():
                gather_far(step, 4 - rel, z).wait_recv()

            u = user_tab[step, chunk, z].reshape(4 * TILE, RANK)
            v = item_tab[step].reshape(ITEM_BLOCKS * TILE, RANK)
            scores = contract(u, v, 1, 1)
            rows = []
            for a in range(4):
                block = a * near_stride + chunk * far_stride + z
                cols = []
                for b in range(ITEM_BLOCKS):
                    k = table_s[0, block * ITEM_BLOCKS + b]
                    score = scores[a * TILE:(a + 1) * TILE, b * TILE:(b + 1) * TILE]
                    err = weights[k].astype(F32) * (score - ratings[k].astype(F32))
                    cols.append(err.astype(BF))
                rows.append(jnp.concatenate(cols, axis=1))
            errors = jnp.concatenate(rows, axis=0)
            user_part = contract(errors, v, 1, 0)
            item_part = contract(u, errors, 0, 0)
            for q in range(4):
                item_grad[q] += item_part[:, q * 512:(q + 1) * 512]

            @pl.when(rel == 0)
            def _():
                grad_own[z] = user_part

            @pl.when(rel > 0)
            def _():
                grad_send[step, rel - 1, z] = user_part.astype(BF)
                reduce_far(step, rel, z).start()

            return carry

        lax.fori_loop(0, 8, part, 0)

        for k in range(2):
            core_send[step, k] = item_grad[2 * k + 1 - core].astype(BF)
        reduce_core(step).start()

        sum_near(step, 0)
        if not last:
            pair_sums(0).start()

        reduce_core(step).wait_recv()
        zl_send[step] = (item_grad[2 - 2 * zlo + core] + core_recv[step, 1 - zlo].astype(F32)).astype(BF)
        reduce_zlo(step).start()
        item_sum[...] = (item_grad[2 * zlo + core] + core_recv[step, zlo].astype(F32)).T

        sum_far(step, 1)
        if not last:
            update_users(0)
            send_users(step + 1, 0)
            sum_near(step, 1)
            pair_sums(1).start()

        reduce_zlo(step).wait_recv()
        item_total = item_sum[...] + zl_recv[step].astype(F32).T
        item_master[...] = item_master[...] - ITEM_RATE * item_total
        if not last:
            send_items(step + 1)
            forward_users(step + 1, 0)
            update_users(1)
            send_users(step + 1, 1)
            gather_items(step + 1, 0).wait_recv()
            gather_items(step + 1, 2).start()
            gather_items(step + 1, 1).wait_recv()
            gather_items(step + 1, 2).wait_recv()
        else:
            store_items.start()
            sum_near(step, 1)
            pair_last().start()
            pair_last().wait_recv()
            mine = near_own[zh, near] + pair_recv[1, zh].astype(F32)
            user_pair[...] = user_master[zh] - USER_RATE * mine
            store_users.start()

    for step in range(STEPS):
        for z in range(2):
            for r in (1, 2, 3):
                gather_near(step, r, z).wait_send()
                gather_far(step, r, z).wait_send()
                reduce_far(step, r, z).wait_send()
                reduce_near(step, r, z).wait_send()
        reduce_core(step).wait_send()
        reduce_zlo(step).wait_send()
        for k in range(3):
            gather_items(step, k).wait_send()
    pair_rows().wait_send()
    pair_sums(0).wait_send()
    pair_sums(1).wait_send()
    pair_last().wait_send()
    store_items.wait()
    store_users.wait()


def per_device(users, items, coords, counts, ratings, weights):
    hbm = pl.BlockSpec(memory_space=pl.ANY)
    dma = pltpu.SemaphoreType.DMA
    return pl.pallas_call(
        kernel,
        name="factorize",
        out_shape=(
            jax.ShapeDtypeStruct(users.shape, F32),
            jax.ShapeDtypeStruct(items.shape, F32),
        ),
        in_specs=[hbm, hbm, hbm, pl.BlockSpec(memory_space=pltpu.SMEM), hbm, hbm],
        out_specs=(hbm, hbm),
        scratch_shapes=[
            pltpu.VMEM((SLOTS + 1, TILE, TILE), BF),
            pltpu.VMEM((SLOTS + 1, TILE, TILE), BF),
            pltpu.VMEM((2, SLOTS), jnp.int32),
            pltpu.VMEM((1, 512), jnp.int32),
            pltpu.SMEM((1, 512), jnp.int32),
            pltpu.VMEM((STEPS, 4, 2, 4, TILE, RANK), BF),
            pltpu.VMEM((STEPS, 4, 512, RANK), BF),
            pltpu.VMEM((TILE, RANK), F32),
            pltpu.VMEM((2, TILE, RANK), F32),
            pltpu.VMEM((512, RANK), F32),
            pltpu.VMEM((STEPS, 3, 2, 512, RANK), BF),
            pltpu.VMEM((2, 512, RANK), F32),
            pltpu.VMEM((STEPS, 3, 2, 512, RANK), BF),
            pltpu.VMEM((STEPS, 2, 4, TILE, RANK), BF),
            pltpu.VMEM((2, 4, TILE, RANK), F32),
            pltpu.VMEM((STEPS, 2, 3, TILE, RANK), BF),
            pltpu.VMEM((STEPS, 2, TILE, RANK), BF),
            pltpu.VMEM((STEPS, 2, TILE, RANK), BF),
            pltpu.VMEM((4, RANK, 512), F32),
            pltpu.VMEM((STEPS, 2, RANK, 512), BF),
            pltpu.VMEM((STEPS, 2, RANK, 512), BF),
            pltpu.VMEM((512, RANK), F32),
            pltpu.VMEM((STEPS, RANK, 512), BF),
            pltpu.VMEM((STEPS, RANK, 512), BF),
            dma((8,)),
            dma((2, 2)), dma((2, 2)),
            dma((STEPS, 3, 2)), dma((STEPS, 3, 2)),
            dma((STEPS, 3, 2)), dma((STEPS, 3, 2)),
            dma((STEPS, 3, 2)), dma((STEPS, 3, 2)),
            dma((STEPS, 3, 2)), dma((STEPS, 3, 2)),
            dma((STEPS,)), dma((STEPS,)),
            dma((STEPS,)), dma((STEPS,)),
            dma((STEPS, 3)), dma((STEPS, 3)),
        ],
        compiler_params=pltpu.CompilerParams(
            collective_id=0, has_side_effects=True, vmem_limit_bytes=60 * 2**20
        ),
        cost_estimate=pl.CostEstimate(
            flops=STEPS * 3 * 2 * 512 * TILE**3, bytes_accessed=2 * SLOTS * TILE * TILE * 2, transcendentals=0
        ),
    )(users, items, jnp.swapaxes(coords, 2, 3), counts, ratings, weights)


def solution(mesh):
    return jax.shard_map(
        per_device,
        mesh=mesh,
        in_specs=(
            P(("users", "items"), None),
            P(("items", "users"), None),
            P("users", "items", None, None),
            P("users", "items"),
            P("users", "items", None, None, None),
            P("users", "items", None, None, None),
        ),
        out_specs=(P(("users", "items"), None), P(("items", "users"), None)),
        check_vma=False,
    )
```

```python
import functools

import jax
import jax.numpy as jnp
from jax import lax
from jax.experimental import pallas as pl
from jax.experimental.pallas import tpu as pltpu
from jax.sharding import PartitionSpec as P

BF = jnp.bfloat16
F32 = jnp.float32
MESH = pl.DeviceIdType.MESH

TILE = 128
RANK = 128
STEPS = 2
SLOTS = 256
ITEM_BLOCKS = 16
USER_RATE = 20.0 / 65536
ITEM_RATE = 20.0 / 16384
LATE = (7, 7)
OWN_FIRST = True


def contract(a, b, da, db):
    return lax.dot_general(a, b, (((da,), (db,)), ((), ())), preferred_element_type=F32)


def kernel(
    users_hbm, items_hbm, coords_hbm, counts_ref, ratings_hbm, weights_hbm,
    new_users_hbm, new_items_hbm,
    ratings, weights, coords, table_v, table_s,
    user_tab, item_tab, user_pair, user_master, item_master,
    grad_send, grad_own, ring_far, near_send, near_own, ring_near, ring_cross, pair_send, pair_recv,
    item_grad, core_send, core_recv, item_sum, zl_send, zl_recv,
    load_sem, pair_ss, pair_rs, agn_ss, agn_rs, agf_ss, agf_rs, rsf_ss, rsf_rs,
    rsn_ss, rsn_rs, rsc_ss, rsc_rs, core_ss, core_rs, zl_ss, zl_rs, agi_ss, agi_rs,
):
    me_u = lax.axis_index("users")
    me_i = lax.axis_index("items")
    core = me_u % 2
    zlo = me_u // 2
    x = me_i // 8
    y = (me_i // 2) % 4
    zh = me_i % 2
    near = x + core * (y - x)
    far = y + core * (x - y)
    near_stride = 8 - 6 * core
    far_stride = 2 + 6 * core

    def near_peer(r):
        return (me_u, me_i + ((near + r) % 4 - near) * near_stride)

    def far_peer(r):
        return (me_u, me_i + ((far + r) % 4 - far) * far_stride)

    def cross_peer(r):
        return (me_u, me_i + ((near + r) % 4 - near) * near_stride + 1 - 2 * zh)

    pair_peer = cross_peer(0)
    core_peer = (me_u + 1 - 2 * core, me_i)
    zlo_peer = (me_u + 2 - 4 * zlo, me_i)

    def remote(src, dst, ss, rs, peer):
        return pltpu.make_async_remote_copy(
            src_ref=src, dst_ref=dst, send_sem=ss, recv_sem=rs, device_id=peer, device_id_type=MESH
        )

    load_items = pltpu.make_async_copy(items_hbm, item_master, load_sem.at[0])
    load_users = pltpu.make_async_copy(users_hbm, user_master.at[zh], load_sem.at[1])
    load_coords = pltpu.make_async_copy(coords_hbm.at[0, 0], coords, load_sem.at[2])
    load_items.start()
    load_users.start()
    load_coords.start()
    loads = (
        pltpu.make_async_copy(ratings_hbm.at[0, 0], ratings.at[pl.ds(0, SLOTS)], load_sem.at[3]),
        pltpu.make_async_copy(weights_hbm.at[0, 0], weights.at[pl.ds(0, SLOTS)], load_sem.at[4]),
    )
    for copy in loads:
        copy.start()
    to_scalars = pltpu.make_async_copy(table_v, table_s, load_sem.at[5])
    store_items = pltpu.make_async_copy(item_master, new_items_hbm, load_sem.at[6])
    store_users = pltpu.make_async_copy(user_pair, new_users_hbm, load_sem.at[7])

    peers = [near_peer(r) for r in (1, 2, 3)] + [far_peer(r) for r in (1, 2, 3)]
    peers += [cross_peer(r) for r in range(4)] + [core_peer, zlo_peer]
    barrier = pltpu.get_barrier_semaphore()
    for peer in peers:
        pl.semaphore_signal(barrier, inc=1, device_id=peer, device_id_type=MESH)
    pl.semaphore_wait(barrier, len(peers))

    def pair_rows():
        return remote(users_hbm, user_pair, pair_ss.at[0, 0], pair_rs.at[0, 0], pair_peer)

    def pair_sums(z):
        return remote(
            pair_send.at[0, z], pair_recv.at[0, z], pair_ss.at[1, z], pair_rs.at[1, z], pair_peer
        )

    def gather_near(step, r, z):
        piece = user_tab.at[step, far, z, near]
        return remote(
            piece, piece, agn_ss.at[step, r - 1, z], agn_rs.at[step, r - 1, z], near_peer(r)
        )

    def gather_far(step, r, z):
        piece = user_tab.at[step, far, z]
        return remote(piece, piece, agf_ss.at[step, r - 1, z], agf_rs.at[step, r - 1, z], far_peer(r))

    def reduce_far(step, r, z):
        return remote(
            grad_send.at[step, r - 1, z], ring_far.at[step, r - 1, z],
            rsf_ss.at[step, r - 1, z], rsf_rs.at[step, r - 1, z], far_peer(r),
        )

    def reduce_near(step, r, z):
        return remote(
            near_send.at[step, z if step + 1 < STEPS else zh, (near + r) % 4], ring_near.at[step, z, r - 1],
            rsn_ss.at[step, r - 1, z], rsn_rs.at[step, r - 1, z], near_peer(r),
        )

    def reduce_cross(r, z):
        return remote(
            near_send.at[1, z, (near + r) % 4], ring_cross.at[r], rsc_ss.at[r], rsc_rs.at[r], cross_peer(r)
        )

    def reduce_core(step):
        return remote(core_send.at[step], core_recv.at[step], core_ss.at[step], core_rs.at[step], core_peer)

    def reduce_zlo(step):
        return remote(zl_send.at[step], zl_recv.at[step], zl_ss.at[step], zl_rs.at[step], zlo_peer)

    def gather_items(step, k):
        quarter = me_u if k < 2 else me_u + 2 - 4 * zlo
        piece = item_tab.at[step, quarter]
        return remote(
            piece, piece, agi_ss.at[step, k], agi_rs.at[step, k], zlo_peer if k == 0 else core_peer
        )

    def send_users(step, z):
        user_tab[step, far, z, near] = user_master[z].astype(BF)
        for r in (2, 1, 3):
            gather_near(step, r, z).start()

    def forward_users(step, z):
        for r in (1, 3, 2):
            gather_near(step, r, z).wait_recv()
        for r in (3, 2, 1):
            gather_far(step, r, z).start()

    def send_items(step):
        item_tab[step, me_u] = item_master[...].astype(BF)
        gather_items(step, 0).start()
        gather_items(step, 1).start()

    def sum_far(step, z):
        for r in (1, 2, 3):
            reduce_far(step, r, z).wait_recv()
        total = grad_own[z]
        for r in range(3):
            total = total + ring_far[step, r, z].astype(F32)
        near_own[z] = total.reshape(4, TILE, RANK)
        near_send[step, z] = total.astype(BF).reshape(4, TILE, RANK)
        if step + 1 < STEPS:
            for r in (2, 1, 3):
                reduce_near(step, r, z).start()
        else:
            @pl.when(zh == z)
            def _():
                for r in (2, 1, 3):
                    reduce_near(step, r, 0).start()

            @pl.when(zh != z)
            def _():
                for r in (2, 1, 3, 0):
                    reduce_cross(r, z).start()

    def sum_near(step, z):
        for r in (1, 3, 2):
            reduce_near(step, r, z).wait_recv()
        total = near_own[z, near]
        for r in range(3):
            total = total + ring_near[step, z, r].astype(F32)
        near_own[z, near] = total
        pair_send[step, z] = total.astype(BF)

    def update_users(z):
        pair_sums(z).wait_recv()
        both = pair_send[0, z].astype(F32) + pair_recv[0, z].astype(F32)
        user_master[z] = user_master[z] - USER_RATE * both

    pair_rows().start()
    load_items.wait()
    send_items(0)

    load_coords.wait()
    cell = coords[0:1] * ITEM_BLOCKS + coords[1:2]
    cell = jnp.where(lax.broadcasted_iota(jnp.int32, (1, SLOTS), 1) < counts_ref[0, 0], cell, -1)
    cell = jnp.broadcast_to(cell, (8, SLOTS)).T[:, 0:1]
    slot = lax.broadcasted_iota(jnp.int32, (SLOTS, 512), 0)
    hit = cell == lax.broadcasted_iota(jnp.int32, (SLOTS, 512), 1)
    table_v[...] = SLOTS + jnp.sum(jnp.where(hit, slot - SLOTS, 0), axis=0, keepdims=True)
    to_scalars.start()
    ratings[SLOTS] = jnp.zeros((TILE, TILE), BF)
    weights[SLOTS] = jnp.zeros((TILE, TILE), BF)

    load_users.wait()
    pair_rows().wait_recv()
    user_master[1 - zh] = user_pair[...]
    for z in range(2):
        send_users(0, z)
    gather_items(0, 0).wait_recv()
    gather_items(0, 2).start()
    for z in range(2):
        forward_users(0, z)
    to_scalars.wait()
    gather_items(0, 1).wait_recv()
    gather_items(0, 2).wait_recv()
    for copy in loads:
        copy.wait()

    for step in range(STEPS):
        last = step + 1 == STEPS
        item_grad[...] = jnp.zeros_like(item_grad)

        def part(c, carry):
            if step == 0 and OWN_FIRST:
                z = jnp.where(c < 2, c, (c - 2) // 3)
                rel = jnp.where(c < 2, 0, (c - 2) % 3 + 1)
            else:
                z = c // 4
                rel = (c % 4 + z) % 4
            chunk = (far + rel) % 4

            if step > 0:
                @pl.when(c == 1)
                def _():
                    forward_users(step, 1)

            @pl.when(c == LATE[step])
            def _():
                sum_far(step, 0)

            @pl.when(rel > 0)
            def _():
                gather_far(step, 4 - rel, z).wait_recv()

            u = user_tab[step, chunk, z].reshape(4 * TILE, RANK)
            v = item_tab[step].reshape(ITEM_BLOCKS * TILE, RANK)
            scores = contract(u, v, 1, 1)
            rows = []
            for a in range(4):
                block = a * near_stride + chunk * far_stride + z
                cols = []
                for b in range(ITEM_BLOCKS):
                    k = table_s[0, block * ITEM_BLOCKS + b]
                    score = scores[a * TILE:(a + 1) * TILE, b * TILE:(b + 1) * TILE]
                    err = weights[k].astype(F32) * (score - ratings[k].astype(F32))
                    cols.append(err.astype(BF))
                rows.append(jnp.concatenate(cols, axis=1))
            errors = jnp.concatenate(rows, axis=0)
            user_part = contract(errors, v, 1, 0)
            item_part = contract(u, errors, 0, 0)
            for q in range(4):
                item_grad[q] += item_part[:, q * 512:(q + 1) * 512]

            @pl.when(rel == 0)
            def _():
                grad_own[z] = user_part

            @pl.when(rel > 0)
            def _():
                grad_send[step, rel - 1, z] = user_part.astype(BF)
                reduce_far(step, rel, z).start()

            return carry

        lax.fori_loop(0, 8, part, 0)

        for k in range(2):
            core_send[step, k] = item_grad[2 * k + 1 - core].astype(BF)
        reduce_core(step).start()

        reduce_core(step).wait_recv()
        zl_send[step] = (item_grad[2 - 2 * zlo + core] + core_recv[step, 1 - zlo].astype(F32)).astype(BF)
        reduce_zlo(step).start()
        item_sum[...] = (item_grad[2 * zlo + core] + core_recv[step, zlo].astype(F32)).T

        if not last:
            sum_near(step, 0)
            pair_sums(0).start()

        sum_far(step, 1)
        if not last:
            update_users(0)
            send_users(step + 1, 0)
            sum_near(step, 1)
            pair_sums(1).start()
        reduce_zlo(step).wait_recv()
        item_total = item_sum[...] + zl_recv[step].astype(F32).T
        item_master[...] = item_master[...] - ITEM_RATE * item_total
        if not last:
            send_items(step + 1)
            forward_users(step + 1, 0)
            update_users(1)
            send_users(step + 1, 1)
            gather_items(step + 1, 0).wait_recv()
            gather_items(step + 1, 2).start()
            gather_items(step + 1, 1).wait_recv()
            gather_items(step + 1, 2).wait_recv()
        else:
            store_items.start()
            mine = near_own[zh, near]
            for r in (1, 3, 2):
                reduce_near(step, r, 0).wait_recv()
                mine = mine + ring_near[step, 0, r - 1].astype(F32)
            for r in (0, 1, 3, 2):
                reduce_cross(r, 1 - zh).wait_recv()
                mine = mine + ring_cross[r].astype(F32)
            user_pair[...] = user_master[zh] - USER_RATE * mine
            store_users.start()

    for step in range(STEPS):
        for z in range(2):
            for r in (1, 2, 3):
                gather_near(step, r, z).wait_send()
                gather_far(step, r, z).wait_send()
                reduce_far(step, r, z).wait_send()
                if step + 1 < STEPS or z == 0:
                    reduce_near(step, r, z).wait_send()
        reduce_core(step).wait_send()
        reduce_zlo(step).wait_send()
        for k in range(3):
            gather_items(step, k).wait_send()
    pair_rows().wait_send()
    pair_sums(0).wait_send()
    pair_sums(1).wait_send()
    for r in range(4):
        reduce_cross(r, 1 - zh).wait_send()
    store_items.wait()
    store_users.wait()


def finish(a_ref, b_ref, c_ref, d_ref):
    c_ref[...] = a_ref[...]
    d_ref[...] = b_ref[...]


def per_device(users, items, coords, counts, ratings, weights):
    hbm = pl.BlockSpec(memory_space=pl.ANY)
    dma = pltpu.SemaphoreType.DMA
    users_out, items_out = pl.pallas_call(
        kernel,
        name="factorize",
        out_shape=(
            jax.ShapeDtypeStruct(users.shape, F32),
            jax.ShapeDtypeStruct(items.shape, F32),
        ),
        in_specs=[hbm, hbm, hbm, pl.BlockSpec(memory_space=pltpu.SMEM), hbm, hbm],
        out_specs=(hbm, hbm),
        scratch_shapes=[
            pltpu.VMEM((SLOTS + 1, TILE, TILE), BF),
            pltpu.VMEM((SLOTS + 1, TILE, TILE), BF),
            pltpu.VMEM((2, SLOTS), jnp.int32),
            pltpu.VMEM((1, 512), jnp.int32),
            pltpu.SMEM((1, 512), jnp.int32),
            pltpu.VMEM((STEPS, 4, 2, 4, TILE, RANK), BF),
            pltpu.VMEM((STEPS, 4, 512, RANK), BF),
            pltpu.VMEM((TILE, RANK), F32),
            pltpu.VMEM((2, TILE, RANK), F32),
            pltpu.VMEM((512, RANK), F32),
            pltpu.VMEM((STEPS, 3, 2, 512, RANK), BF),
            pltpu.VMEM((2, 512, RANK), F32),
            pltpu.VMEM((STEPS, 3, 2, 512, RANK), BF),
            pltpu.VMEM((STEPS, 2, 4, TILE, RANK), BF),
            pltpu.VMEM((2, 4, TILE, RANK), F32),
            pltpu.VMEM((STEPS, 2, 3, TILE, RANK), BF),
            pltpu.VMEM((4, TILE, RANK), BF),
            pltpu.VMEM((STEPS, 2, TILE, RANK), BF),
            pltpu.VMEM((STEPS, 2, TILE, RANK), BF),
            pltpu.VMEM((4, RANK, 512), F32),
            pltpu.VMEM((STEPS, 2, RANK, 512), BF),
            pltpu.VMEM((STEPS, 2, RANK, 512), BF),
            pltpu.VMEM((512, RANK), F32),
            pltpu.VMEM((STEPS, RANK, 512), BF),
            pltpu.VMEM((STEPS, RANK, 512), BF),
            dma((8,)),
            dma((2, 2)), dma((2, 2)),
            dma((STEPS, 3, 2)), dma((STEPS, 3, 2)),
            dma((STEPS, 3, 2)), dma((STEPS, 3, 2)),
            dma((STEPS, 3, 2)), dma((STEPS, 3, 2)),
            dma((STEPS, 3, 2)), dma((STEPS, 3, 2)),
            dma((4,)), dma((4,)),
            dma((STEPS,)), dma((STEPS,)),
            dma((STEPS,)), dma((STEPS,)),
            dma((STEPS, 3)), dma((STEPS, 3)),
        ],
        compiler_params=pltpu.CompilerParams(
            collective_id=0, has_side_effects=True, vmem_limit_bytes=60 * 2**20
        ),
        cost_estimate=pl.CostEstimate(
            flops=STEPS * 3 * 2 * 512 * TILE**3, bytes_accessed=2 * SLOTS * TILE * TILE * 2, transcendentals=0
        ),
    )(users, items, jnp.swapaxes(coords, 2, 3), counts, ratings, weights)
    vmem = pl.BlockSpec(memory_space=pltpu.VMEM)
    return pl.pallas_call(
        finish,
        name="finish",
        out_shape=(
            jax.ShapeDtypeStruct(users.shape, F32),
            jax.ShapeDtypeStruct(items.shape, F32),
        ),
        in_specs=[vmem, vmem],
        out_specs=(vmem, vmem),
    )(users_out, items_out)


def solution(mesh):
    return jax.shard_map(
        per_device,
        mesh=mesh,
        in_specs=(
            P(("users", "items"), None),
            P(("items", "users"), None),
            P("users", "items", None, None),
            P("users", "items"),
            P("users", "items", None, None, None),
            P("users", "items", None, None, None),
        ),
        out_specs=(P(("users", "items"), None), P(("items", "users"), None)),
        check_vma=False,
    )
```

```python
import functools

import jax
import jax.numpy as jnp
from jax import lax
from jax.experimental import pallas as pl
from jax.experimental.pallas import tpu as pltpu
from jax.sharding import PartitionSpec as P

BF = jnp.bfloat16
F32 = jnp.float32
MESH = pl.DeviceIdType.MESH

TILE = 128
RANK = 128
STEPS = 2
SLOTS = 256
ITEM_BLOCKS = 16
USER_RATE = 20.0 / 65536
ITEM_RATE = 20.0 / 16384
LATE = (7, 7)
OWN_FIRST = True


def contract(a, b, da, db):
    return lax.dot_general(a, b, (((da,), (db,)), ((), ())), preferred_element_type=F32)


def kernel(
    users_hbm, items_hbm, coords_hbm, counts_ref, ratings_hbm, weights_hbm,
    new_users_hbm, new_items_hbm,
    ratings, weights, coords, table_v, table_s,
    user_tab, item_tab, user_pair, user_master, item_master,
    grad_send, grad_own, ring_far, near_send, near_own, ring_near, ring_cross, ring_both,
    item_grad, core_send, core_recv, item_sum, zl_send, zl_recv,
    load_sem, pair_ss, pair_rs, agn_ss, agn_rs, agf_ss, agf_rs, agb_ss, agb_rs, rsf_ss, rsf_rs,
    rsn_ss, rsn_rs, rsc_ss, rsc_rs, rsb_ss, rsb_rs, core_ss, core_rs, zl_ss, zl_rs, agi_ss, agi_rs,
):
    me_u = lax.axis_index("users")
    me_i = lax.axis_index("items")
    core = me_u % 2
    zlo = me_u // 2
    x = me_i // 8
    y = (me_i // 2) % 4
    zh = me_i % 2
    near = x + core * (y - x)
    far = y + core * (x - y)
    near_stride = 8 - 6 * core
    far_stride = 2 + 6 * core

    def near_peer(r):
        return (me_u, me_i + ((near + r) % 4 - near) * near_stride)

    def far_peer(r):
        return (me_u, me_i + ((far + r) % 4 - far) * far_stride)

    def cross_peer(r):
        return (me_u, me_i + ((near + r) % 4 - near) * near_stride + 1 - 2 * zh)

    pair_peer = cross_peer(0)
    core_peer = (me_u + 1 - 2 * core, me_i)
    zlo_peer = (me_u + 2 - 4 * zlo, me_i)

    def remote(src, dst, ss, rs, peer):
        return pltpu.make_async_remote_copy(
            src_ref=src, dst_ref=dst, send_sem=ss, recv_sem=rs, device_id=peer, device_id_type=MESH
        )

    load_items = pltpu.make_async_copy(items_hbm, item_master, load_sem.at[0])
    load_users = pltpu.make_async_copy(users_hbm, user_master.at[zh], load_sem.at[1])
    load_coords = pltpu.make_async_copy(coords_hbm.at[0, 0], coords, load_sem.at[2])
    load_items.start()
    load_users.start()
    load_coords.start()
    loads = (
        pltpu.make_async_copy(ratings_hbm.at[0, 0], ratings.at[pl.ds(0, SLOTS)], load_sem.at[3]),
        pltpu.make_async_copy(weights_hbm.at[0, 0], weights.at[pl.ds(0, SLOTS)], load_sem.at[4]),
    )
    for copy in loads:
        copy.start()
    to_scalars = pltpu.make_async_copy(table_v, table_s, load_sem.at[5])
    store_items = pltpu.make_async_copy(item_master, new_items_hbm, load_sem.at[6])
    store_users = pltpu.make_async_copy(user_pair, new_users_hbm, load_sem.at[7])

    peers = [near_peer(r) for r in (1, 2, 3)] + [far_peer(r) for r in (1, 2, 3)]
    peers += [cross_peer(r) for r in range(4)] + [core_peer, zlo_peer]
    barrier = pltpu.get_barrier_semaphore()
    for peer in peers:
        pl.semaphore_signal(barrier, inc=1, device_id=peer, device_id_type=MESH)
    pl.semaphore_wait(barrier, len(peers))

    def pair_rows():
        return remote(users_hbm, user_pair, pair_ss.at[0, 0], pair_rs.at[0, 0], pair_peer)

    def reduce_both(z, w, r):
        mine = zh * 4 + near
        return remote(
            near_send.at[0, z, (near + r) % 4], ring_both.at[z, mine],
            rsb_ss.at[z, w * 4 + r], rsb_rs.at[z, mine], cross_peer(r) if w else near_peer(r),
        )

    def from_both(z, w, r):
        source = (zh + w) % 2 * 4 + (near + 4 - r) % 4
        return remote(
            near_send.at[0, z, (near + r) % 4], ring_both.at[z, source],
            rsb_ss.at[z, w * 4 + r], rsb_rs.at[z, source], cross_peer(r) if w else near_peer(r),
        )

    def gather_near(step, r, z):
        piece = user_tab.at[step, far, z, near]
        return remote(
            piece, piece, agn_ss.at[step, r - 1, z], agn_rs.at[step, r - 1, z], near_peer(r)
        )

    def gather_both(w, r):
        piece = user_tab.at[0, far, zh, near]
        k = w * 4 + r
        return remote(
            piece, piece, agb_ss.at[k], agb_rs.at[k], cross_peer(r) if w else near_peer(r)
        )

    def gather_far(step, r, z):
        piece = user_tab.at[step, far, z]
        return remote(piece, piece, agf_ss.at[step, r - 1, z], agf_rs.at[step, r - 1, z], far_peer(r))

    def reduce_far(step, r, z):
        return remote(
            grad_send.at[step, r - 1, z], ring_far.at[step, r - 1, z],
            rsf_ss.at[step, r - 1, z], rsf_rs.at[step, r - 1, z], far_peer(r),
        )

    def reduce_near(step, r, z):
        return remote(
            near_send.at[step, z if step + 1 < STEPS else zh, (near + r) % 4], ring_near.at[step, z, r - 1],
            rsn_ss.at[step, r - 1, z], rsn_rs.at[step, r - 1, z], near_peer(r),
        )

    def reduce_cross(r, z):
        return remote(
            near_send.at[1, z, (near + r) % 4], ring_cross.at[r], rsc_ss.at[r], rsc_rs.at[r], cross_peer(r)
        )

    def reduce_core(step):
        return remote(core_send.at[step], core_recv.at[step], core_ss.at[step], core_rs.at[step], core_peer)

    def reduce_zlo(step):
        return remote(zl_send.at[step], zl_recv.at[step], zl_ss.at[step], zl_rs.at[step], zlo_peer)

    def gather_items(step, k):
        quarter = me_u if k < 2 else me_u + 2 - 4 * zlo
        piece = item_tab.at[step, quarter]
        return remote(
            piece, piece, agi_ss.at[step, k], agi_rs.at[step, k], zlo_peer if k == 0 else core_peer
        )

    def send_users(step, z):
        user_tab[step, far, z, near] = user_master[z].astype(BF)
        for r in (2, 1, 3):
            gather_near(step, r, z).start()

    def forward_users(step, z):
        if step > 0:
            for r in (1, 3, 2):
                gather_near(step, r, z).wait_recv()
        else:
            @pl.when(zh == z)
            def _():
                for r in (1, 3, 2):
                    gather_both(0, r).wait_recv()

            @pl.when(zh != z)
            def _():
                for r in (0, 1, 3, 2):
                    gather_both(1, r).wait_recv()

        for r in (3, 2, 1):
            gather_far(step, r, z).start()

    def send_items(step):
        item_tab[step, me_u] = item_master[...].astype(BF)
        gather_items(step, 0).start()
        gather_items(step, 1).start()

    def sum_far(step, z):
        for r in (1, 2, 3):
            reduce_far(step, r, z).wait_recv()
        total = grad_own[z]
        for r in range(3):
            total = total + ring_far[step, r, z].astype(F32)
        near_own[z] = total.reshape(4, TILE, RANK)
        near_send[step, z] = total.astype(BF).reshape(4, TILE, RANK)
        if step + 1 < STEPS:
            ring_both[z, zh * 4 + near] = near_send[0, z, near]
            for r in (2, 1, 3, 0):
                reduce_both(z, 1, r).start()
            for r in (2, 1, 3):
                reduce_both(z, 0, r).start()
        else:
            @pl.when(zh == z)
            def _():
                for r in (2, 1, 3):
                    reduce_near(step, r, 0).start()

            @pl.when(zh != z)
            def _():
                for r in (2, 1, 3, 0):
                    reduce_cross(r, z).start()

    def update_users(z):
        for r in (1, 3, 2):
            from_both(z, 0, r).wait_recv()
        for r in (0, 1, 3, 2):
            from_both(z, 1, r).wait_recv()
        total = ring_both[z, 0].astype(F32)
        for k in range(1, 8):
            total = total + ring_both[z, k].astype(F32)
        user_master[z] = user_master[z] - USER_RATE * total

    load_users.wait()
    user_tab[0, far, zh, near] = user_master[zh].astype(BF)
    for r in (2, 1, 3, 0):
        gather_both(1, r).start()
    for r in (2, 1, 3):
        gather_both(0, r).start()
    load_items.wait()
    send_items(0)

    load_coords.wait()
    cell = coords[0:1] * ITEM_BLOCKS + coords[1:2]
    cell = jnp.where(lax.broadcasted_iota(jnp.int32, (1, SLOTS), 1) < counts_ref[0, 0], cell, -1)
    cell = jnp.broadcast_to(cell, (8, SLOTS)).T[:, 0:1]
    slot = lax.broadcasted_iota(jnp.int32, (SLOTS, 512), 0)
    hit = cell == lax.broadcasted_iota(jnp.int32, (SLOTS, 512), 1)
    table_v[...] = SLOTS + jnp.sum(jnp.where(hit, slot - SLOTS, 0), axis=0, keepdims=True)
    to_scalars.start()
    ratings[SLOTS] = jnp.zeros((TILE, TILE), BF)
    weights[SLOTS] = jnp.zeros((TILE, TILE), BF)

    gather_items(0, 0).wait_recv()
    gather_items(0, 2).start()
    for z in range(2):
        forward_users(0, z)
    pair_rows().start()
    to_scalars.wait()
    gather_items(0, 1).wait_recv()
    gather_items(0, 2).wait_recv()
    for copy in loads:
        copy.wait()

    for step in range(STEPS):
        last = step + 1 == STEPS
        item_grad[...] = jnp.zeros_like(item_grad)

        def part(c, carry):
            if step == 0 and OWN_FIRST:
                z = jnp.where(c < 2, c, (c - 2) // 3)
                rel = jnp.where(c < 2, 0, (c - 2) % 3 + 1)
            else:
                z = c // 4
                rel = (c % 4 + z) % 4
            chunk = (far + rel) % 4

            if step > 0:
                @pl.when(c == 1)
                def _():
                    forward_users(step, 1)

            @pl.when(c == LATE[step])
            def _():
                sum_far(step, 0)

            @pl.when(rel > 0)
            def _():
                gather_far(step, 4 - rel, z).wait_recv()

            u = user_tab[step, chunk, z].reshape(4 * TILE, RANK)
            v = item_tab[step].reshape(ITEM_BLOCKS * TILE, RANK)
            scores = contract(u, v, 1, 1)
            rows = []
            for a in range(4):
                block = a * near_stride + chunk * far_stride + z
                cols = []
                for b in range(ITEM_BLOCKS):
                    k = table_s[0, block * ITEM_BLOCKS + b]
                    score = scores[a * TILE:(a + 1) * TILE, b * TILE:(b + 1) * TILE]
                    err = weights[k].astype(F32) * (score - ratings[k].astype(F32))
                    cols.append(err.astype(BF))
                rows.append(jnp.concatenate(cols, axis=1))
            errors = jnp.concatenate(rows, axis=0)
            user_part = contract(errors, v, 1, 0)
            item_part = contract(u, errors, 0, 0)
            for q in range(4):
                item_grad[q] += item_part[:, q * 512:(q + 1) * 512]

            @pl.when(rel == 0)
            def _():
                grad_own[z] = user_part

            @pl.when(rel > 0)
            def _():
                grad_send[step, rel - 1, z] = user_part.astype(BF)
                reduce_far(step, rel, z).start()

            return carry

        lax.fori_loop(0, 8, part, 0)

        for k in range(2):
            core_send[step, k] = item_grad[2 * k + 1 - core].astype(BF)
        reduce_core(step).start()

        reduce_core(step).wait_recv()
        zl_send[step] = (item_grad[2 - 2 * zlo + core] + core_recv[step, 1 - zlo].astype(F32)).astype(BF)
        reduce_zlo(step).start()
        item_sum[...] = (item_grad[2 * zlo + core] + core_recv[step, zlo].astype(F32)).T

        sum_far(step, 1)
        if not last:
            pair_rows().wait_recv()
            user_master[1 - zh] = user_pair[...]
            update_users(0)
            send_users(step + 1, 0)
        reduce_zlo(step).wait_recv()
        item_total = item_sum[...] + zl_recv[step].astype(F32).T
        item_master[...] = item_master[...] - ITEM_RATE * item_total
        if not last:
            send_items(step + 1)
            forward_users(step + 1, 0)
            update_users(1)
            send_users(step + 1, 1)
            gather_items(step + 1, 0).wait_recv()
            gather_items(step + 1, 2).start()
            gather_items(step + 1, 1).wait_recv()
            gather_items(step + 1, 2).wait_recv()
        else:
            store_items.start()
            mine = near_own[zh, near]
            for r in (1, 3, 2):
                reduce_near(step, r, 0).wait_recv()
                mine = mine + ring_near[step, 0, r - 1].astype(F32)
            for r in (0, 1, 3, 2):
                reduce_cross(r, 1 - zh).wait_recv()
                mine = mine + ring_cross[r].astype(F32)
            user_pair[...] = user_master[zh] - USER_RATE * mine
            store_users.start()

    for step in range(STEPS):
        for z in range(2):
            for r in (1, 2, 3):
                if step > 0:
                    gather_near(step, r, z).wait_send()
                gather_far(step, r, z).wait_send()
                reduce_far(step, r, z).wait_send()
                if step + 1 < STEPS:
                    reduce_both(z, 0, r).wait_send()
                elif z == 0:
                    reduce_near(step, r, z).wait_send()
        reduce_core(step).wait_send()
        reduce_zlo(step).wait_send()
        for k in range(3):
            gather_items(step, k).wait_send()
    pair_rows().wait_send()
    for k in range(1, 8):
        gather_both(k // 4, k % 4).wait_send()
    for z in range(2):
        for r in range(4):
            reduce_both(z, 1, r).wait_send()
    for r in range(4):
        reduce_cross(r, 1 - zh).wait_send()
    store_items.wait()
    store_users.wait()


def finish(a_ref, b_ref, c_ref, d_ref):
    c_ref[...] = a_ref[...]
    d_ref[...] = b_ref[...]


def per_device(users, items, coords, counts, ratings, weights):
    hbm = pl.BlockSpec(memory_space=pl.ANY)
    dma = pltpu.SemaphoreType.DMA
    users_out, items_out = pl.pallas_call(
        kernel,
        name="factorize",
        out_shape=(
            jax.ShapeDtypeStruct(users.shape, F32),
            jax.ShapeDtypeStruct(items.shape, F32),
        ),
        in_specs=[hbm, hbm, hbm, pl.BlockSpec(memory_space=pltpu.SMEM), hbm, hbm],
        out_specs=(hbm, hbm),
        scratch_shapes=[
            pltpu.VMEM((SLOTS + 1, TILE, TILE), BF),
            pltpu.VMEM((SLOTS + 1, TILE, TILE), BF),
            pltpu.VMEM((2, SLOTS), jnp.int32),
            pltpu.VMEM((1, 512), jnp.int32),
            pltpu.SMEM((1, 512), jnp.int32),
            pltpu.VMEM((STEPS, 4, 2, 4, TILE, RANK), BF),
            pltpu.VMEM((STEPS, 4, 512, RANK), BF),
            pltpu.VMEM((TILE, RANK), F32),
            pltpu.VMEM((2, TILE, RANK), F32),
            pltpu.VMEM((512, RANK), F32),
            pltpu.VMEM((STEPS, 3, 2, 512, RANK), BF),
            pltpu.VMEM((2, 512, RANK), F32),
            pltpu.VMEM((STEPS, 3, 2, 512, RANK), BF),
            pltpu.VMEM((STEPS, 2, 4, TILE, RANK), BF),
            pltpu.VMEM((2, 4, TILE, RANK), F32),
            pltpu.VMEM((STEPS, 2, 3, TILE, RANK), BF),
            pltpu.VMEM((4, TILE, RANK), BF),
            pltpu.VMEM((2, 8, TILE, RANK), BF),
            pltpu.VMEM((4, RANK, 512), F32),
            pltpu.VMEM((STEPS, 2, RANK, 512), BF),
            pltpu.VMEM((STEPS, 2, RANK, 512), BF),
            pltpu.VMEM((512, RANK), F32),
            pltpu.VMEM((STEPS, RANK, 512), BF),
            pltpu.VMEM((STEPS, RANK, 512), BF),
            dma((8,)),
            dma((2, 2)), dma((2, 2)),
            dma((STEPS, 3, 2)), dma((STEPS, 3, 2)),
            dma((STEPS, 3, 2)), dma((STEPS, 3, 2)),
            dma((8,)), dma((8,)),
            dma((STEPS, 3, 2)), dma((STEPS, 3, 2)),
            dma((STEPS, 3, 2)), dma((STEPS, 3, 2)),
            dma((4,)), dma((4,)),
            dma((2, 8)), dma((2, 8)),
            dma((STEPS,)), dma((STEPS,)),
            dma((STEPS,)), dma((STEPS,)),
            dma((STEPS, 3)), dma((STEPS, 3)),
        ],
        compiler_params=pltpu.CompilerParams(
            collective_id=0, has_side_effects=True, vmem_limit_bytes=60 * 2**20
        ),
        cost_estimate=pl.CostEstimate(
            flops=STEPS * 3 * 2 * 512 * TILE**3, bytes_accessed=2 * SLOTS * TILE * TILE * 2, transcendentals=0
        ),
    )(users, items, jnp.swapaxes(coords, 2, 3), counts, ratings, weights)
    vmem = pl.BlockSpec(memory_space=pltpu.VMEM)
    return pl.pallas_call(
        finish,
        name="finish",
        out_shape=(
            jax.ShapeDtypeStruct(users.shape, F32),
            jax.ShapeDtypeStruct(items.shape, F32),
        ),
        in_specs=[vmem, vmem],
        out_specs=(vmem, vmem),
    )(users_out, items_out)


def solution(mesh):
    return jax.shard_map(
        per_device,
        mesh=mesh,
        in_specs=(
            P(("users", "items"), None),
            P(("items", "users"), None),
            P("users", "items", None, None),
            P("users", "items"),
            P("users", "items", None, None, None),
            P("users", "items", None, None, None),
        ),
        out_specs=(P(("users", "items"), None), P(("items", "users"), None)),
        check_vma=False,
    )
```
